256 devices in a mesh: blk: 64 (over z, y, core), layer: 4 (over x).
Axes of the slice: x: 4, y: 4, z: 8, core: 2. Of those that a mesh axis runs over, the one named last changes fastest.
Arguments:
- leaf_area: float32 [12, 16, 8192], P(None, 'layer', 'blk'), may hold values from 0 to 6
- soil_water: float32 [10, 8192], P(None, 'blk'), may hold values from 0.05 to 0.5
- root_share: float32 [16, 10], P('layer'), may hold values from 0 to 0.3
- patch_weight: float32 [16, 262144], P('layer', 'blk'), may hold values from 0 to 1
- patch_owner: int32 [262144, 1], P('blk'), may hold values from 0 to 63; in each aligned block of 4096 rows (0 to 4095, 4096 to 8191, ...) at most 128 rows name the same one
- patch_local: int32 [262144], P('blk'), may hold values from 0 to 127
- month: int32 [1], replicated, may hold values from 0 to 11
- mix: float32 [1], replicated, may hold values from 0.1 to 0.9
Outputs:
- canopy_share: float32 [16, 8192], P('layer', 'blk')
The draws below stay inside these ranges and needn't reach their ends.
Inputs may be any that keep to these rules, and one draw needn't show every extreme that they name: `patch_owner`: among the rows of one device, no owner is named more than 128 times, a bound that some block reaches.
All inputs are finite; a program needn't handle non-finite values.
Results may differ from the reference program's by a relative error of at most 0.000065.
Values sent between devices are 32-bit elements; how exact they have to be, the bound alone decides.
No kernel may reach another device: no remote copies, remote signals or barrier semaphores. Data moves between devices by JAX's collectives and lax.ppermute only.
A program may use at most 64 MiB of HBM per device.

```python
import math
import jax
import jax.numpy as jnp
import numpy as np
from jax import lax

PFT = 16
MONTHS = 12
SOIL = 10
G_DEV = 128
P_DEV = 4096
GRID = 8192
PATCHES = 262144
CAP = 128
N_BLK = 64


def touch_ends(drawn, rng, low, top_value):
    spot = [jax.random.randint(jax.random.fold_in(rng, axis), (), 0, length) for axis, length in enumerate(drawn.shape)]
    longest = drawn.shape.index(max(drawn.shape))
    next_to = spot[:longest] + [(spot[longest] + 1) % drawn.shape[longest]] + spot[longest + 1:]
    return drawn.at[tuple(spot)].set(low).at[tuple(next_to)].set(top_value)


def level_of(own_key, extent, pieces, low, top_value):
    def one(axis_at, parts):
        steps = jax.random.uniform(jax.random.fold_in(jax.random.fold_in(own_key, 6), axis_at), (parts,), jnp.float32, low / len(pieces), top_value / len(pieces))
        return jnp.repeat(jnp.exp(steps), extent[axis_at] // parts).reshape((-1,) + (1,) * (len(extent) - axis_at - 1))

    gain = one(*pieces[0])
    for cut in pieces[1:]:
        gain = gain * one(*cut)
    return gain


def assign_block(stream_key, own, number, rows, count, top, most, skew):
    ranking = jax.random.permutation(stream_key, count)
    heavy_load, usual = load_shares(count, rows * top, most, skew, True), load_shares(count, rows * top, most, skew, False)
    places = jnp.arange(count)

    def named(lengths, rotation):
        used = int((lengths > 0).sum())
        fixed = max(1, used // 4)
        passed = fixed + (places - fixed + rotation * (used - fixed)) % max(1, count - fixed)
        return jnp.zeros((count,), jnp.int32).at[ranking[jnp.where(places < fixed, places, passed)]].set(jnp.asarray(lengths, jnp.int32))

    lengths = jnp.where(number % 4 == 0, named(heavy_load, number // 4), named(usual, number - number // 4 - 1))
    mixed = jax.random.permutation(jax.random.fold_in(own, 3), count)
    source_of, receiver = mixed[0:count // 2 * 2:2], mixed[1:count // 2 * 2:2]
    margin = jnp.minimum(lengths[source_of] - 1, most - lengths[receiver]) // 2
    margin = jnp.where((source_of == ranking[0]) | (receiver == ranking[0]) | (lengths[receiver] == 0), 0, jnp.maximum(margin, 0))
    passed = jax.random.randint(jax.random.fold_in(own, 4), (count // 2,), 0, 1 << 20) % (margin + 1)
    lengths = lengths.at[source_of].add(-passed).at[receiver].add(passed)
    items = jnp.searchsorted(jnp.cumsum(lengths), jnp.arange(rows * top), side="right").astype(jnp.int32)
    table = items.reshape(top, rows).T
    table = table[jax.random.permutation(jax.random.fold_in(own, 1), rows)]
    rotation = jax.random.randint(jax.random.fold_in(own, 2), (rows, 1), 0, top)
    return jnp.take_along_axis(table, (jnp.arange(top)[None, :] + rotation) % top, axis=1)


def load_shares(count, total, reach, skew, full):
    weights = [(1 << 20) // math.isqrt(standing ** skew) + 1 for standing in range(1, count + 1)]
    largest = reach if full else min(reach, max(-(-total // count), total * weights[0] // sum(weights)))
    least = 1 if total - largest >= count - 1 else 0
    counts, surplus = [largest] + [least] * (count - 1), total - largest - least * (count - 1)
    while surplus > 0:
        free = [i for i in range(1, count) if counts[i] < largest] or [i for i in range(1, count) if counts[i] < reach]
        mass, left = sum([weights[i] for i in free]), surplus
        for i in free:
            addition = min(reach - counts[i], max(1, left * weights[i] // mass), surplus)
            counts[i] = counts[i] + addition
            surplus = surplus - addition
    return np.array(counts)


def setup_inputs(seed: int = 0) -> dict:
    keys = jax.random.split(jax.random.key(seed), 9)
    leaf_area = jnp.clip(6.0 * jax.random.uniform(keys[0], (MONTHS, PFT, GRID), jnp.float32) ** level_of(keys[0], (MONTHS, PFT, GRID), ((1, 4), (2, 64)), -0.2, 0.2), 0.0, 6.0)
    soil_water = jnp.clip(0.05 + 0.45 * jax.random.uniform(keys[1], (SOIL, GRID), jnp.float32) ** level_of(keys[1], (SOIL, GRID), ((1, 64),), -0.2, 0.2), 0.05, 0.5)
    root_share = jnp.clip(0.3 * jax.random.uniform(keys[2], (PFT, SOIL), jnp.float32) ** level_of(keys[2], (PFT, SOIL), ((0, 4),), -0.2, 0.2), 0.0, 0.3)
    patch_weight = jnp.clip(1.0 * jax.random.uniform(keys[3], (PFT, PATCHES), jnp.float32) ** level_of(keys[3], (PFT, PATCHES), ((0, 4), (1, 64)), -0.2, 0.2), 0.0, 1.0)
    patch_owner_keys = jax.random.split(jax.random.fold_in(keys[4], 1), PATCHES // P_DEV)
    patch_owner_turns = jax.random.permutation(jax.random.fold_in(keys[4], 3), PATCHES // P_DEV)
    patch_owner = jax.vmap(lambda own, number: assign_block(jax.random.fold_in(keys[4], 2), own, number, P_DEV, N_BLK, 1, CAP, 2))(patch_owner_keys, patch_owner_turns).reshape((PATCHES, 1))
    patch_local = touch_ends(jax.random.randint(keys[5], (PATCHES,), 0, G_DEV), jax.random.fold_in(keys[5], 1), 0, G_DEV - 1).astype(jnp.int32)
    month = jax.random.randint(keys[6], (1,), 0, MONTHS).astype(jnp.int32)
    mix = jnp.clip(jax.random.uniform(keys[7], (1,), jnp.float32, 0.1, 0.9), 0.1, 0.9)
    return dict(leaf_area=leaf_area, soil_water=soil_water, root_share=root_share, patch_weight=patch_weight, patch_owner=patch_owner, patch_local=patch_local, month=month, mix=mix)


def interpolate(leaf_area, month, mix):
    earlier_index = month[0]
    second = (earlier_index + 1) % MONTHS
    earlier = lax.dynamic_index_in_dim(leaf_area, earlier_index, 0, keepdims=False)
    later = lax.dynamic_index_in_dim(leaf_area, second, 0, keepdims=False)
    return mix[0] * earlier + (1.0 - mix[0]) * later


def reference(leaf_area, soil_water, root_share, patch_weight, patch_owner, patch_local, month, mix):
    patch_cell = (patch_owner[:, 0] * G_DEV + patch_local).astype(jnp.int32)
    current = interpolate(leaf_area, month, mix)
    patch_leaf = jnp.take(current, patch_cell, axis=1)
    patch_soil = jnp.take(soil_water, patch_cell, axis=1)
    stress = jnp.dot(root_share, patch_soil, precision=lax.Precision.HIGHEST)
    canopy = patch_weight * (1.0 - jnp.exp(-0.5 * patch_leaf)) * stress
    grid_sum = jax.ops.segment_sum(canopy.T, patch_cell, num_segments=GRID).T
    total = jnp.sum(grid_sum, axis=0)
    return grid_sum / (1.0 + total)
```

```python
import jax
import jax.numpy as jnp
from jax import lax
from jax.experimental import pallas as pl
from jax.experimental.pallas import tpu as pltpu
from jax.sharding import Mesh
from jax.sharding import PartitionSpec as P

F32 = jnp.float32
BF16 = jnp.bfloat16
CHUNK = 256
CELLS = 128


def vmem():
    return pl.BlockSpec(memory_space=pltpu.VMEM)


def limit(mib):
    return pltpu.CompilerParams(vmem_limit_bytes=mib << 20)


def smem():
    return pl.BlockSpec(memory_space=pltpu.SMEM)


def weight_sums_kernel(core_ref, weight_ref, owner_ref, local_ref, send_ref, keep_ref):
    types, patches = weight_ref.shape
    rows = send_ref.shape[0]
    chips = rows // types
    row_chip = lax.broadcasted_iota(jnp.int32, (rows, CHUNK), 0) // types
    row_chip = row_chip.astype(F32).astype(BF16)
    column = lax.broadcasted_iota(jnp.int32, (2 * CELLS, CHUNK), 0).astype(F32).astype(BF16)
    zero = jnp.zeros((), BF16)
    one = jnp.ones((), BF16)
    total = jnp.zeros((2 * rows, 2 * CELLS), F32)
    for step in range(patches // CHUNK):
        part = pl.ds(step * CHUNK, CHUNK)
        owner = owner_ref[:, part]
        chip = (owner >> 1).astype(F32).astype(BF16)
        place = ((owner & 1) * CELLS + local_ref[:, part]).astype(F32).astype(BF16)
        weight = weight_ref[:, part]
        high = weight.astype(BF16)
        low = (weight - high.astype(F32)).astype(BF16)
        named = jnp.broadcast_to(chip, (rows, CHUNK)) == row_chip
        left = jnp.concatenate(
            [
                jnp.where(named, jnp.concatenate([high] * chips, axis=0), zero),
                jnp.where(named, jnp.concatenate([low] * chips, axis=0), zero),
            ],
            axis=0,
        )
        right = jnp.where(jnp.broadcast_to(place, (2 * CELLS, CHUNK)) == column, one, zero)
        total += lax.dot_general(
            left, right, (((1,), (1,)), ((), ())), preferred_element_type=F32
        )
    both = total[:rows] + total[rows:]
    first, second = both[:, :CELLS], both[:, CELLS:]
    low_core = core_ref[0] == 0
    send_ref[...] = jnp.where(low_core, second, first)
    keep_ref[...] = jnp.where(low_core, first, second)


def weight_sums(core, weight, owner, local, chips):
    types, patches = weight.shape
    shape = jax.ShapeDtypeStruct((chips * types, CELLS), F32)
    return pl.pallas_call(
        weight_sums_kernel,
        out_shape=[shape, shape],
        in_specs=[smem(), vmem(), vmem(), vmem()],
        out_specs=[vmem(), vmem()],
        compiler_params=limit(8),
        name="weight_sums",
    )(core, weight, owner, local)


def factor_kernel(month_ref, mix_ref, leaf_ref, soil_ref, root_ref, factor_ref):
    earlier = month_ref[0]
    later = (earlier + 1) % leaf_ref.shape[0]
    mix = mix_ref[0]
    current = mix * leaf_ref[earlier] + (1.0 - mix) * leaf_ref[later]
    stress = jnp.zeros_like(current)
    for layer in range(soil_ref.shape[0]):
        stress += root_ref[:, layer : layer + 1] * soil_ref[layer : layer + 1, :]
    factor_ref[...] = (1.0 - jnp.exp(-0.5 * current)) * stress


def cell_factor(month, mix, leaf_area, soil_water, root_share):
    return pl.pallas_call(
        factor_kernel,
        out_shape=jax.ShapeDtypeStruct(leaf_area.shape[1:], F32),
        in_specs=[smem(), smem(), vmem(), vmem(), vmem()],
        out_specs=vmem(),
        compiler_params=limit(1),
        name="cell_factor",
    )(month, mix, leaf_area, soil_water, root_share)


def grid_sum_kernel(received_ref, factor_ref, grid_sum_ref, total_ref):
    grid_sum = jnp.sum(received_ref[...], axis=0) * factor_ref[...]
    grid_sum_ref[...] = grid_sum
    total_ref[...] = jnp.sum(grid_sum, axis=0, keepdims=True)


def share_kernel(grid_sum_ref, total_ref, *rest):
    *others, share_ref = rest
    total = total_ref[...]
    for other in others:
        total += other[...]
    share_ref[...] = grid_sum_ref[...] / (1.0 + total)


def on_device(
    leaf_area, soil_water, root_share, patch_weight, patch_owner, patch_local, month, mix
):
    types = leaf_area.shape[1]
    chips = lax.axis_size("z") * lax.axis_size("y")
    layers = lax.axis_size("x")
    core = lax.axis_index("core").astype(jnp.int32).reshape(1)
    send, keep = weight_sums(
        core, patch_weight, patch_owner.reshape(1, -1), patch_local.reshape(1, -1), chips
    )
    sums = keep + lax.ppermute(send, "core", [(0, 1), (1, 0)])
    received = lax.all_to_all(
        sums.reshape(chips, types, CELLS), ("z", "y"), split_axis=0, concat_axis=0, tiled=True
    )
    factor = cell_factor(month, mix, leaf_area, soil_water, root_share)
    grid_sum, total = pl.pallas_call(
        grid_sum_kernel,
        out_shape=[
            jax.ShapeDtypeStruct((types, CELLS), F32),
            jax.ShapeDtypeStruct((1, CELLS), F32),
        ],
        in_specs=[vmem(), vmem()],
        out_specs=[vmem(), vmem()],
        compiler_params=limit(1),
        name="grid_sum",
    )(received, factor)
    others = [
        lax.ppermute(total, "x", [(i, (i + hop) % layers) for i in range(layers)])
        for hop in range(1, layers)
    ]
    return pl.pallas_call(
        share_kernel,
        out_shape=jax.ShapeDtypeStruct((types, CELLS), F32),
        in_specs=[vmem()] * (1 + layers),
        out_specs=vmem(),
        compiler_params=limit(1),
        name="canopy_share",
    )(grid_sum, total, *others)


def solution(mesh):
    blk = ("z", "y", "core")
    inner = Mesh(mesh.devices.reshape(8, 4, 2, 4), (*blk, "x"))
    in_specs = (
        P(None, "x", blk),
        P(None, blk),
        P("x", None),
        P("x", blk),
        P(blk, None),
        P(blk),
        P(),
        P(),
    )
    return jax.shard_map(
        on_device, mesh=inner, in_specs=in_specs, out_specs=P("x", blk), check_vma=False
    )
```

```python
import jax
import jax.numpy as jnp
from jax import lax
from jax.experimental import pallas as pl
from jax.experimental.pallas import tpu as pltpu
from jax.sharding import PartitionSpec as P

F32 = jnp.float32
BF16 = jnp.bfloat16
CHUNK = 256
CELLS = 128


def vmem():
    return pl.BlockSpec(memory_space=pltpu.VMEM)


def smem():
    return pl.BlockSpec(memory_space=pltpu.SMEM)


def hbm():
    return pl.BlockSpec(memory_space=pltpu.HBM)


def limit(mib):
    return pltpu.CompilerParams(vmem_limit_bytes=mib << 20)


def load(pairs, sems):
    copies = [pltpu.make_async_copy(a, b, sems.at[i]) for i, (a, b) in enumerate(pairs)]
    for copy in copies:
        copy.start()
    return copies


def weight_sums_kernel(
    core_ref, weight_hbm, owner_hbm, local_hbm, send_ref, keep_ref,
    weight_ref, owner_ref, local_ref, sems,
):
    copies = load(
        [(weight_hbm, weight_ref), (owner_hbm, owner_ref), (local_hbm, local_ref)], sems
    )
    types, patches = weight_ref.shape
    rows = send_ref.shape[0]
    chips = rows // types
    row_chip = (lax.broadcasted_iota(jnp.int32, (rows, CHUNK), 0) // types + 22) % chips
    row_chip = row_chip.astype(F32).astype(BF16)
    column = lax.broadcasted_iota(jnp.int32, (2 * CELLS, CHUNK), 0).astype(F32).astype(BF16)
    zero = jnp.zeros((), BF16)
    one = jnp.ones((), BF16)
    total = jnp.zeros((2 * rows, 2 * CELLS), F32)
    for copy in copies:
        copy.wait()
    for step in range(patches // CHUNK):
        part = pl.ds(step * CHUNK, CHUNK)
        owner = owner_ref[:, part]
        chip = (owner >> 1).astype(F32).astype(BF16)
        place = ((owner & 1) * CELLS + local_ref[:, part]).astype(F32).astype(BF16)
        weight = weight_ref[:, part]
        high = weight.astype(BF16)
        low = (weight - high.astype(F32)).astype(BF16)
        named = jnp.broadcast_to(chip, (rows, CHUNK)) == row_chip
        left = jnp.concatenate(
            [
                jnp.where(named, jnp.concatenate([high] * chips, axis=0), zero),
                jnp.where(named, jnp.concatenate([low] * chips, axis=0), zero),
            ],
            axis=0,
        )
        right = jnp.where(jnp.broadcast_to(place, (2 * CELLS, CHUNK)) == column, one, zero)
        total += lax.dot_general(
            left, right, (((1,), (1,)), ((), ())), preferred_element_type=F32
        )
    both = total[:rows] + total[rows:]
    first, second = both[:, :CELLS], both[:, CELLS:]
    low_core = core_ref[0] == 0
    send_ref[...] = jnp.where(low_core, second, first)
    keep_ref[...] = jnp.where(low_core, first, second)


def weight_sums(core, arrays, chips):
    types = arrays[0].shape[0]
    shape = jax.ShapeDtypeStruct((chips * types, CELLS), F32)
    return pl.pallas_call(
        weight_sums_kernel,
        out_shape=[shape, shape],
        in_specs=[smem()] + [hbm()] * len(arrays),
        out_specs=[vmem()] * 2,
        scratch_shapes=[pltpu.VMEM(a.shape, a.dtype) for a in arrays]
        + [pltpu.SemaphoreType.DMA((len(arrays),))],
        compiler_params=limit(8),
        name="weight_sums",
    )(core, *[pltpu.with_memory_space_constraint(a, pltpu.HBM) for a in arrays])


def factor_kernel(month_ref, mix_ref, leaf_ref, soil_ref, root_ref, factor_ref):
    earlier = month_ref[0]
    later = jnp.where(earlier == leaf_ref.shape[0] - 1, 0, earlier + 1)
    mix = mix_ref[0]
    current = mix * leaf_ref[earlier] + (1.0 - mix) * leaf_ref[later]
    stress = jnp.zeros_like(current)
    for layer in range(soil_ref.shape[0]):
        stress += root_ref[:, layer : layer + 1] * soil_ref[layer : layer + 1, :]
    factor_ref[...] = (1.0 - jnp.exp(-0.5 * current)) * stress


def cell_factor(month, mix, leaf_area, soil_water, root_share):
    return pl.pallas_call(
        factor_kernel,
        out_shape=jax.ShapeDtypeStruct(leaf_area.shape[1:], F32),
        in_specs=[smem(), smem(), vmem(), vmem(), vmem()],
        out_specs=vmem(),
        compiler_params=limit(1),
        cost_estimate=pl.CostEstimate(flops=20000, transcendentals=512, bytes_accessed=40000),
        name="cell_factor",
    )(month, mix, leaf_area, soil_water, root_share)


def grid_sum_kernel(received_ref, factor_ref, grid_sum_ref, total_ref):
    grid_sum = jnp.sum(received_ref[...], axis=0) * factor_ref[...]
    grid_sum_ref[...] = grid_sum
    total_ref[...] = jnp.broadcast_to(jnp.sum(grid_sum, axis=0, keepdims=True)[None], total_ref.shape)


def share_kernel(grid_sum_ref, totals_ref, share_ref):
    share_ref[...] = grid_sum_ref[...] / (1.0 + jnp.sum(totals_ref[...], axis=0))


def on_device(
    leaf_area, soil_water, root_share, patch_weight, patch_owner, patch_local, month, mix
):
    types = leaf_area.shape[1]
    devices = lax.axis_size("blk")
    chips = devices // 2
    layers = lax.axis_size("layer")
    core = (lax.axis_index("blk").astype(jnp.int32) & 1).reshape(1)
    send, keep = weight_sums(
        core, [patch_weight, patch_owner.reshape(1, -1), patch_local.reshape(1, -1)], chips
    )
    factor = cell_factor(month, mix, leaf_area, soil_water, root_share)
    sums = keep + lax.ppermute(send, "blk", [(i, i ^ 1) for i in range(devices)])
    sums, factor = lax.optimization_barrier((sums, factor))
    received = lax.all_to_all(
        sums.reshape(chips, types, CELLS), "blk", split_axis=0, concat_axis=0, tiled=True,
        axis_index_groups=[
            [(i + 22) % chips * 2 + half for i in range(chips)] for half in range(2)
        ],
    )
    grid_sum, total = pl.pallas_call(
        grid_sum_kernel,
        out_shape=[
            jax.ShapeDtypeStruct((types, CELLS), F32),
            jax.ShapeDtypeStruct((layers, 1, CELLS), F32),
        ],
        in_specs=[vmem(), vmem()],
        out_specs=[vmem(), vmem()],
        compiler_params=limit(1),
        name="grid_sum",
    )(received, factor)
    totals = lax.all_to_all(
        total, "layer", split_axis=0, concat_axis=0, tiled=True,
        axis_index_groups=[[(i + 2) % layers for i in range(layers)]],
    )
    operands = [grid_sum, totals]
    return pl.pallas_call(
        share_kernel,
        out_shape=jax.ShapeDtypeStruct((types, CELLS), F32),
        in_specs=[vmem()] * len(operands),
        out_specs=vmem(),
        compiler_params=limit(1),
        name="canopy_share",
    )(*operands)


def solution(mesh):
    in_specs = (
        P(None, "layer", "blk"),
        P(None, "blk"),
        P("layer", None),
        P("layer", "blk"),
        P("blk", None),
        P("blk"),
        P(),
        P(),
    )
    return jax.shard_map(
        on_device, mesh=mesh, in_specs=in_specs, out_specs=P("layer", "blk"), check_vma=False
    )
```

```python
import jax
import jax.numpy as jnp
from jax import lax
from jax.experimental import pallas as pl
from jax.experimental.pallas import tpu as pltpu
from jax.sharding import PartitionSpec as P

F32 = jnp.float32
BF16 = jnp.bfloat16
CHUNK = 256
CELLS = 128


def vmem():
    return pl.BlockSpec(memory_space=pltpu.VMEM)


def smem():
    return pl.BlockSpec(memory_space=pltpu.SMEM)


def hbm():
    return pl.BlockSpec(memory_space=pltpu.HBM)


def limit(mib):
    return pltpu.CompilerParams(vmem_limit_bytes=mib << 20)


def load(pairs, sems):
    copies = [pltpu.make_async_copy(a, b, sems.at[i]) for i, (a, b) in enumerate(pairs)]
    for copy in copies:
        copy.start()
    return copies


def weight_sums_kernel(
    core_ref, weight_hbm, owner_hbm, local_hbm, send_ref, keep_ref,
    weight_ref, owner_ref, local_ref, sems,
):
    copies = load(
        [(weight_hbm, weight_ref), (owner_hbm, owner_ref), (local_hbm, local_ref)], sems
    )
    types, patches = weight_ref.shape
    rows = send_ref.shape[0]
    chips = rows // types
    row_chip = (lax.broadcasted_iota(jnp.int32, (rows, CHUNK), 0) // types + 22) % chips
    row_chip = row_chip.astype(F32).astype(BF16)
    column = lax.broadcasted_iota(jnp.int32, (2 * CELLS, CHUNK), 0).astype(F32).astype(BF16)
    zero = jnp.zeros((), BF16)
    one = jnp.ones((), BF16)
    total = jnp.zeros((2 * rows, 2 * CELLS), F32)
    for copy in copies:
        copy.wait()
    for step in range(patches // CHUNK):
        part = pl.ds(step * CHUNK, CHUNK)
        owner = owner_ref[:, part]
        chip = (owner >> 1).astype(F32).astype(BF16)
        place = ((owner & 1) * CELLS + local_ref[:, part]).astype(F32).astype(BF16)
        weight = weight_ref[:, part]
        high = weight.astype(BF16)
        low = (weight - high.astype(F32)).astype(BF16)
        named = jnp.broadcast_to(chip, (rows, CHUNK)) == row_chip
        left = jnp.concatenate(
            [
                jnp.where(named, jnp.concatenate([high] * chips, axis=0), zero),
                jnp.where(named, jnp.concatenate([low] * chips, axis=0), zero),
            ],
            axis=0,
        )
        right = jnp.where(jnp.broadcast_to(place, (2 * CELLS, CHUNK)) == column, one, zero)
        total += lax.dot_general(
            left, right, (((1,), (1,)), ((), ())), preferred_element_type=F32
        )
    both = total[:rows] + total[rows:]
    first, second = both[:, :CELLS], both[:, CELLS:]
    low_core = core_ref[0] == 0
    send_ref[...] = jnp.where(low_core, second, first)
    keep_ref[...] = jnp.where(low_core, first, second)


def weight_sums(core, arrays, chips):
    types = arrays[0].shape[0]
    shape = jax.ShapeDtypeStruct((chips * types, CELLS), F32)
    return pl.pallas_call(
        weight_sums_kernel,
        out_shape=[shape, shape],
        in_specs=[smem()] + [hbm()] * len(arrays),
        out_specs=[vmem()] * 2,
        scratch_shapes=[pltpu.VMEM(a.shape, a.dtype) for a in arrays]
        + [pltpu.SemaphoreType.DMA((len(arrays),))],
        compiler_params=limit(8),
        name="weight_sums",
    )(core, *[pltpu.with_memory_space_constraint(a, pltpu.HBM) for a in arrays])


def factor_kernel(month_ref, mix_ref, leaf_ref, soil_ref, root_ref, factor_ref):
    earlier = month_ref[0]
    later = jnp.where(earlier == leaf_ref.shape[0] - 1, 0, earlier + 1)
    mix = mix_ref[0]
    current = mix * leaf_ref[earlier] + (1.0 - mix) * leaf_ref[later]
    stress = jnp.zeros_like(current)
    for layer in range(soil_ref.shape[0]):
        stress += root_ref[:, layer : layer + 1] * soil_ref[layer : layer + 1, :]
    factor_ref[...] = (1.0 - jnp.exp(-0.5 * current)) * stress


def cell_factor(month, mix, leaf_area, soil_water, root_share):
    return pl.pallas_call(
        factor_kernel,
        out_shape=jax.ShapeDtypeStruct(leaf_area.shape[1:], F32),
        in_specs=[smem(), smem(), vmem(), vmem(), vmem()],
        out_specs=vmem(),
        compiler_params=limit(1),
        cost_estimate=pl.CostEstimate(flops=20000, transcendentals=512, bytes_accessed=40000),
        name="cell_factor",
    )(month, mix, leaf_area, soil_water, root_share)


def grid_sum_kernel(received_ref, factor_ref, grid_sum_ref, total_ref):
    grid_sum = jnp.sum(received_ref[...], axis=0) * factor_ref[...]
    grid_sum_ref[...] = grid_sum
    total_ref[...] = jnp.sum(grid_sum, axis=0, keepdims=True)


def share_kernel(grid_sum_ref, total_ref, *rest):
    *others, share_ref = rest
    total = total_ref[...]
    for other in others:
        total += other[...]
    share_ref[...] = grid_sum_ref[...] / (1.0 + total)


def on_device(
    leaf_area, soil_water, root_share, patch_weight, patch_owner, patch_local, month, mix
):
    types = leaf_area.shape[1]
    devices = lax.axis_size("blk")
    chips = devices // 2
    layers = lax.axis_size("layer")
    core = (lax.axis_index("blk").astype(jnp.int32) & 1).reshape(1)
    send, keep = weight_sums(
        core, [patch_weight, patch_owner.reshape(1, -1), patch_local.reshape(1, -1)], chips
    )
    factor = cell_factor(month, mix, leaf_area, soil_water, root_share)
    sums = keep + lax.ppermute(send, "blk", [(i, i ^ 1) for i in range(devices)])
    sums, factor = lax.optimization_barrier((sums, factor))
    received = lax.all_to_all(
        sums.reshape(chips, types, CELLS), "blk", split_axis=0, concat_axis=0, tiled=True,
        axis_index_groups=[
            [(i + 22) % chips * 2 + half for i in range(chips)] for half in range(2)
        ],
    )
    grid_sum, total = pl.pallas_call(
        grid_sum_kernel,
        out_shape=[
            jax.ShapeDtypeStruct((types, CELLS), F32),
            jax.ShapeDtypeStruct((1, CELLS), F32),
        ],
        in_specs=[vmem(), vmem()],
        out_specs=[vmem(), vmem()],
        compiler_params=limit(1),
        name="grid_sum",
    )(received, factor)
    others = [
        lax.ppermute(total, "layer", pairs) for pairs in [[(0, 3), (1, 2), (2, 0), (3, 1)], [(0, 2), (1, 3), (2, 1), (3, 0)], [(0, 1), (1, 0), (2, 3), (3, 2)]]
    ]
    operands = [grid_sum, total, *others]
    return pl.pallas_call(
        share_kernel,
        out_shape=jax.ShapeDtypeStruct((types, CELLS), F32),
        in_specs=[vmem()] * len(operands),
        out_specs=vmem(),
        compiler_params=limit(1),
        name="canopy_share",
    )(*operands)


def solution(mesh):
    in_specs = (
        P(None, "layer", "blk"),
        P(None, "blk"),
        P("layer", None),
        P("layer", "blk"),
        P("blk", None),
        P("blk"),
        P(),
        P(),
    )
    return jax.shard_map(
        on_device, mesh=mesh, in_specs=in_specs, out_specs=P("layer", "blk"), check_vma=False
    )
```

```python
import jax
import jax.numpy as jnp
from jax import lax
from jax.experimental import pallas as pl
from jax.experimental.pallas import tpu as pltpu
from jax.sharding import PartitionSpec as P

F32 = jnp.float32
BF16 = jnp.bfloat16
CHUNK = 256
CELLS = 128


def vmem():
    return pl.BlockSpec(memory_space=pltpu.VMEM)


def smem():
    return pl.BlockSpec(memory_space=pltpu.SMEM)


def hbm():
    return pl.BlockSpec(memory_space=pltpu.HBM)


def limit(mib):
    return pltpu.CompilerParams(vmem_limit_bytes=mib << 20)


def load(pairs, sems):
    copies = [pltpu.make_async_copy(a, b, sems.at[i]) for i, (a, b) in enumerate(pairs)]
    for copy in copies:
        copy.start()
    return copies


def weight_sums_kernel(
    core_ref, weight_hbm, owner_hbm, local_hbm, send_ref, keep_ref,
    weight_ref, owner_ref, local_ref, sems,
):
    copies = load(
        [(weight_hbm, weight_ref), (owner_hbm, owner_ref), (local_hbm, local_ref)], sems
    )
    types, patches = weight_ref.shape
    rows = send_ref.shape[0]
    chips = rows // types
    row_chip = (lax.broadcasted_iota(jnp.int32, (rows, CHUNK), 0) // types + 22) % chips
    row_chip = row_chip.astype(F32).astype(BF16)
    column = lax.broadcasted_iota(jnp.int32, (2 * CELLS, CHUNK), 0).astype(F32).astype(BF16)
    zero = jnp.zeros((), BF16)
    one = jnp.ones((), BF16)
    total = jnp.zeros((2 * rows, 2 * CELLS), F32)
    for copy in copies:
        copy.wait()
    for step in range(patches // CHUNK):
        part = pl.ds(step * CHUNK, CHUNK)
        owner = owner_ref[:, part]
        chip = (owner >> 1).astype(F32).astype(BF16)
        place = ((owner & 1) * CELLS + local_ref[:, part]).astype(F32).astype(BF16)
        weight = weight_ref[:, part]
        high = weight.astype(BF16)
        low = (weight - high.astype(F32)).astype(BF16)
        named = jnp.broadcast_to(chip, (rows, CHUNK)) == row_chip
        left = jnp.concatenate(
            [
                jnp.where(named, jnp.concatenate([high] * chips, axis=0), zero),
                jnp.where(named, jnp.concatenate([low] * chips, axis=0), zero),
            ],
            axis=0,
        )
        right = jnp.where(jnp.broadcast_to(place, (2 * CELLS, CHUNK)) == column, one, zero)
        total += lax.dot_general(
            left, right, (((1,), (1,)), ((), ())), preferred_element_type=F32
        )
    both = total[:rows] + total[rows:]
    first, second = both[:, :CELLS], both[:, CELLS:]
    low_core = core_ref[0] == 0
    send_ref[...] = jnp.where(low_core, second, first)
    keep_ref[...] = jnp.where(low_core, first, second)


def weight_sums(core, arrays, chips):
    types = arrays[0].shape[0]
    shape = jax.ShapeDtypeStruct((chips * types, CELLS), F32)
    return pl.pallas_call(
        weight_sums_kernel,
        out_shape=[shape, shape],
        in_specs=[smem()] + [hbm()] * len(arrays),
        out_specs=[vmem()] * 2,
        scratch_shapes=[pltpu.VMEM(a.shape, a.dtype) for a in arrays]
        + [pltpu.SemaphoreType.DMA((len(arrays),))],
        compiler_params=limit(8),
        name="weight_sums",
    )(core, *[pltpu.with_memory_space_constraint(a, pltpu.HBM) for a in arrays])


def factor_kernel(month_ref, mix_ref, leaf_ref, soil_ref, root_ref, factor_ref):
    earlier = month_ref[0]
    later = jnp.where(earlier == leaf_ref.shape[0] - 1, 0, earlier + 1)
    mix = mix_ref[0]
    current = mix * leaf_ref[earlier] + (1.0 - mix) * leaf_ref[later]
    stress = jnp.zeros_like(current)
    for layer in range(soil_ref.shape[0]):
        stress += root_ref[:, layer : layer + 1] * soil_ref[layer : layer + 1, :]
    factor_ref[...] = (1.0 - jnp.exp(-0.5 * current)) * stress


def cell_factor(month, mix, leaf_area, soil_water, root_share):
    return pl.pallas_call(
        factor_kernel,
        out_shape=jax.ShapeDtypeStruct(leaf_area.shape[1:], F32),
        in_specs=[smem(), smem(), vmem(), vmem(), vmem()],
        out_specs=vmem(),
        compiler_params=limit(1),
        cost_estimate=pl.CostEstimate(flops=20000, transcendentals=512, bytes_accessed=40000),
        name="cell_factor",
    )(month, mix, leaf_area, soil_water, root_share)


def grid_sum_kernel(received_ref, factor_ref, grid_sum_ref, total_ref):
    grid_sum = jnp.sum(received_ref[...], axis=0) * factor_ref[...]
    grid_sum_ref[...] = grid_sum
    total_ref[...] = jnp.sum(grid_sum, axis=0, keepdims=True)


def share_kernel(grid_sum_ref, total_ref, *rest):
    *others, share_ref = rest
    total = total_ref[...]
    for other in others:
        total += other[...]
    share_ref[...] = grid_sum_ref[...] / (1.0 + total)


def on_device(
    leaf_area, soil_water, root_share, patch_weight, patch_owner, patch_local, month, mix
):
    types = leaf_area.shape[1]
    devices = lax.axis_size("blk")
    chips = devices // 2
    layers = lax.axis_size("layer")
    core = (lax.axis_index("blk").astype(jnp.int32) & 1).reshape(1)
    send, keep = weight_sums(
        core, [patch_weight, patch_owner.reshape(1, -1), patch_local.reshape(1, -1)], chips
    )
    factor = cell_factor(month, mix, leaf_area, soil_water, root_share)
    sums = keep + lax.ppermute(send, "blk", [(i, i ^ 1) for i in range(devices)])
    sums, factor = lax.optimization_barrier((sums, factor))
    received = lax.all_to_all(
        sums.reshape(chips, types, CELLS), "blk", split_axis=0, concat_axis=0, tiled=True,
        axis_index_groups=[
            [(i + 22) % chips * 2 + half for i in range(chips)] for half in range(2)
        ],
    )
    grid_sum, total = pl.pallas_call(
        grid_sum_kernel,
        out_shape=[
            jax.ShapeDtypeStruct((types, CELLS), F32),
            jax.ShapeDtypeStruct((1, CELLS), F32),
        ],
        in_specs=[vmem(), vmem()],
        out_specs=[vmem(), vmem()],
        compiler_params=limit(1),
        name="grid_sum",
    )(received, factor)
    orders = ((3, 2, 0, 1), (2, 3, 1, 0), (1, 0, 3, 2))
    others = [
        lax.ppermute(
            total,
            ("blk", "layer"),
            [
                (i * layers + x, i * layers + orders[(step + i % 2 * 2) % 3][x])
                for i in range(devices)
                for x in range(layers)
            ],
        )
        for step in range(3)
    ]
    operands = [grid_sum, total, *others]
    return pl.pallas_call(
        share_kernel,
        out_shape=jax.ShapeDtypeStruct((types, CELLS), F32),
        in_specs=[vmem()] * len(operands),
        out_specs=vmem(),
        compiler_params=limit(1),
        name="canopy_share",
    )(*operands)


def solution(mesh):
    in_specs = (
        P(None, "layer", "blk"),
        P(None, "blk"),
        P("layer", None),
        P("layer", "blk"),
        P("blk", None),
        P("blk"),
        P(),
        P(),
    )
    return jax.shard_map(
        on_device, mesh=mesh, in_specs=in_specs, out_specs=P("layer", "blk"), check_vma=False
    )
```
